32 devices in a mesh: obs: 4 (over y, x), bfly: 8 (over z, core).
Axes of the slice: x: 2, y: 2, z: 4, core: 2. Of those that a mesh axis runs over, the one named last changes fastest.
Arguments:
- obs_field: float32 [32768, 1024], P(('obs', 'bfly')), may hold values from -6 to 6
- observer_leaf_bases: float32 [64, 512, 256], P(('obs', 'bfly')), may hold values from -0.25 to 0.25
- transfer: float32 [3, 64, 256, 512], P(None, ('obs', 'bfly')), may hold values from -0.25 to 0.25
- src_basis: float32 [16, 512, 256], P('bfly'), may hold values from -0.375 to 0.375
- leaf_map: int32 [4, 8], replicated, may hold values from 0 to 3, as said below
- partner_perm: int32 [3, 256], replicated, may hold values from 0 to 255, each once within a row
Outputs:
- src_field: float32 [1024, 8192], P('obs', 'bfly')
The draws below stay inside these ranges and needn't reach their ends.
Inputs may be any that keep to these rules, and one draw needn't show every extreme that they name: In every column b, leaf_map[o, b] = (o + r_b) mod 4 for one offset r_b of that column, so each column names every observer group once. `partner_perm`: each row is a permutation of the rank indices.
All inputs are finite; a program needn't handle non-finite values.
Results may differ from the reference program's by a relative error of at most 0.0001.
Values sent between devices are 32-bit elements; how exact they have to be, the bound alone decides.
A program may use at most 64 MiB of HBM per device.

```python
import jax
import jax.numpy as jnp
from jax import lax

LEAF = 512
RANK = 256
COLS = 1024
NODES_DEV = 2
LEVELS = 3
OBS_NODES = 64
SRC_NODES = 16
ROWS = 32768
N_OBS = 4
N_BFLY = 8


def draw_leaf_map(key, part):
    offsets = jax.random.randint(key, (N_BFLY,), 0, N_OBS, dtype=jnp.int32)
    group_index = jnp.arange(N_OBS, dtype=jnp.int32)
    return (group_index[:, None] + offsets[None, :]) % N_OBS


def steps_of(own_key, extent, shards, smallest, top_value):
    gain = 1.0
    for position, parts in shards:
        steps = jax.random.uniform(jax.random.fold_in(jax.random.fold_in(own_key, 6), position), (parts,), jnp.float32, smallest / len(shards), top_value / len(shards))
        gain = gain * jnp.repeat(jnp.exp(steps), extent[position] // parts).reshape((-1,) + (1,) * (len(extent) - 1 - position))
    return gain


def noise(own_key, extent, width, most, cuts=(), held_as=jnp.bfloat16):
    values = jax.random.normal(own_key, extent, jnp.float32) * width
    if len(cuts) > 0:
        values = steps_of(own_key, extent, cuts, -0.22, 0.18) * values
    return jnp.clip(values, min=-most, max=most).astype(held_as)


def setup_inputs(seed: int = 0) -> dict:
    streams_of = jax.random.split(jax.random.key(seed), 7)
    obs_field = noise(streams_of[0], (ROWS, COLS), 1.0, 6.0, ((0, 32),), jnp.float32)
    observer_leaf_bases = noise(streams_of[1], (OBS_NODES, LEAF, RANK), LEAF ** -0.5, 0.25, ((0, 32),), jnp.float32)
    transfer = noise(streams_of[2], (LEVELS, OBS_NODES, RANK, 2 * RANK), (2 * RANK) ** -0.5, 0.25, ((1, 32),), jnp.float32)
    src_basis = noise(streams_of[3], (SRC_NODES, LEAF, RANK), RANK ** -0.5, 0.375, ((0, 8),), jnp.float32)
    leaf_map = draw_leaf_map(jax.random.fold_in(streams_of[6], 71), 0)
    partner_perm = jax.vmap(lambda own: jax.random.permutation(own, RANK))(jax.random.split(streams_of[5], LEVELS)).reshape((LEVELS, RANK)).astype(jnp.int32)
    return {"obs_field": obs_field, "observer_leaf_bases": observer_leaf_bases, "transfer": transfer, "src_basis": src_basis, "leaf_map": leaf_map, "partner_perm": partner_perm}


def reference(obs_field, observer_leaf_bases, transfer, src_basis, leaf_map, partner_perm):
    highest_level = lax.Precision.HIGHEST
    groups = N_OBS * N_BFLY * NODES_DEV
    block_list = obs_field.reshape(groups, LEAF, COLS)
    projected_field = jnp.einsum('hft,hfm->htm', observer_leaf_bases, block_list, precision=highest_level)
    projected_field = projected_field.reshape(N_OBS, N_BFLY, NODES_DEV, RANK, COLS)
    columns = jnp.arange(N_BFLY, dtype=jnp.int32)
    carried = projected_field[leaf_map, columns[None, :]]
    transfers = transfer.reshape(LEVELS, N_OBS, N_BFLY, NODES_DEV, RANK, 2 * RANK)
    for level_index in range(LEVELS):
        partner = carried[:, columns ^ (1 << level_index)]
        partner = jnp.take(partner, partner_perm[level_index], axis=3)
        joined = jnp.concatenate([carried, partner], axis=3)
        carried = jnp.einsum('objrs,objsc->objrc', transfers[level_index], joined, precision=highest_level)
    summed = jnp.sum(carried, axis=0)
    source_basis = src_basis.reshape(N_BFLY, NODES_DEV, LEAF, RANK)
    result = jnp.einsum('bjlr,bjrc->cbjl', source_basis, summed, precision=highest_level)
    return result.reshape(COLS, N_BFLY * NODES_DEV * LEAF)
```

```python
import jax
import jax.numpy as jnp
from jax import lax
from jax.sharding import PartitionSpec as P

HIGH = lax.Precision.HIGH


def swapped(block, axis, apart):
    count = lax.axis_size(axis)
    return lax.ppermute(block, axis, [(i, i ^ apart) for i in range(count)])


def dot(spec, a, b):
    return jnp.einsum(spec, a, b, precision=HIGH, preferred_element_type=jnp.float32)


def body(obs_field, observer_leaf_bases, transfer, src_basis, leaf_map, partner_perm):
    node_count, leaf_rows, rank_size = observer_leaf_bases.shape
    col_count = obs_field.shape[1]
    level_count = transfer.shape[0]
    groups = lax.axis_size("obs")
    share = col_count // groups
    me = lax.axis_index("obs")
    bfly_index = lax.axis_index("bfly")
    ranks = jnp.arange(rank_size, dtype=jnp.int32)

    near, far = [], []
    for k in range(level_count):
        onehot = (partner_perm[k][:, None] == ranks[None, :]).astype(jnp.float32)
        near.append(transfer[k, :, :, :rank_size])
        far.append(dot("jri,im->jrm", transfer[k, :, :, rank_size:], onehot))
    last = level_count - 1
    far_last = swapped(far[last], "bfly", 1 << last)

    blocks = obs_field.reshape(node_count, leaf_rows, col_count)
    arrived = []
    for k in range(groups):
        piece = lax.dynamic_slice_in_dim(blocks, (me ^ k) * share, share, 2)
        projected = dot("jlr,jlc->jrc", observer_leaf_bases, piece)
        arrived.append(projected if k == 0 else swapped(projected, "obs", k))
    stack = jnp.stack(arrived)
    chunks = []
    for k in range(groups):
        source = leaf_map[me ^ k, bfly_index]
        pick = lax.dynamic_index_in_dim(stack, source ^ me, 0, keepdims=False)
        chunks.append(pick if k == 0 else swapped(pick, "obs", k))

    total = None
    total_far = None
    for k in range(groups):
        carried = chunks[k]
        for level in range(last):
            partner = swapped(carried, "bfly", 1 << level)
            carried = dot("jrs,jsc->jrc", near[level], carried) + dot(
                "jrs,jsc->jrc", far[level], partner
            )
        away = dot("jrs,jsc->jrc", far_last, carried)
        own = dot("jrs,jsc->jrc", near[last], carried)
        if k:
            away = swapped(away, "obs", k)
            own = swapped(own, "obs", k)
        total_far = away if total_far is None else total_far + away
        total = own if total is None else total + own
    summed = total + swapped(total_far, "bfly", 1 << last)
    parts = [dot("rc,lr->cl", summed[j], src_basis[j]) for j in range(node_count)]
    return jnp.concatenate(parts, axis=1)


def solution(mesh):
    placed = (
        P(("obs", "bfly"), None),
        P(("obs", "bfly"), None, None),
        P(None, ("obs", "bfly"), None, None),
        P("bfly", None, None),
        P(),
        P(),
    )
    return jax.shard_map(
        body, mesh=mesh, in_specs=placed, out_specs=P("obs", "bfly"), check_vma=False
    )
```

```python
import functools

import jax
import jax.numpy as jnp
from jax import lax
from jax.experimental import pallas as pl
from jax.experimental.pallas import tpu as pltpu
from jax.sharding import PartitionSpec as P

MESH = pl.DeviceIdType.MESH
EXACT = lax.Precision.HIGHEST


def mm(a, b, rhs_dim=0):
    return lax.dot_general(
        a,
        b,
        (((1,), (rhs_dim,)), ((), ())),
        precision=EXACT,
        preferred_element_type=jnp.float32,
    )


def flip(index, bits):
    out = index
    for shift in range(3):
        unit = 1 << shift
        out = out + unit * ((bits // unit) % 2) * (1 - 2 * ((index // unit) % 2))
    return out


def kernel(
    groups,
    obs_ref,
    bases_ref,
    transfer_ref,
    src_ref,
    perm_ref,
    map_ref,
    out_ref,
    turned,
    far,
    far_away,
    send_a,
    send_b,
    cur,
    got,
    send_r,
    got_r,
    send_f,
    got_f,
    sem_w,
    sem_a,
    sem_b,
    sem_x,
    sem_r,
    sem_f,
    *arrived,
):
    nodes, leaf, rank = bases_ref.shape
    levels = transfer_ref.shape[0]
    last = levels - 1
    share = obs_ref.shape[1] // groups
    me = lax.axis_index("obs")
    col = lax.axis_index("bfly")

    def over_obs(k):
        return (flip(me, k), col)

    def over_bfly(level):
        unit = 1 << level
        return (me, col + unit * (1 - 2 * ((col // unit) % 2)))

    def remote(src, dst, sems, index, device):
        return pltpu.make_async_remote_copy(
            src_ref=src,
            dst_ref=dst,
            send_sem=sems.at[(0, *index)],
            recv_sem=sems.at[(1, *index)],
            device_id=device,
            device_id_type=MESH,
        )

    def copy_a(j, k):
        return remote(send_a.at[j, k], arrived[j].at[me], sem_a, (j, k), over_obs(k))

    def copy_b(j, k):
        return remote(send_b.at[j, k], cur.at[0, j, k], sem_b, (j, k), over_obs(k))

    def copy_x(level, j, k):
        return remote(
            cur.at[level, j, k], got.at[level, j, k], sem_x, (level, j, k), over_bfly(level)
        )

    def copy_r(which, j, k):
        return remote(
            send_r.at[which, j, k], got_r.at[which, j, k], sem_r, (which, j, k), over_obs(k)
        )

    def copy_f(j):
        return remote(send_f.at[j], got_f.at[j], sem_f, (j,), over_bfly(last))

    copy_w = remote(far.at[last], far_away, sem_w, (0,), over_bfly(last))

    barrier = pltpu.get_barrier_semaphore()
    for k in range(1, groups):
        pl.semaphore_signal(barrier, inc=1, device_id=over_obs(k), device_id_type=MESH)
    for level in range(levels):
        pl.semaphore_signal(barrier, inc=1, device_id=over_bfly(level), device_id_type=MESH)
    pl.semaphore_wait(barrier, groups - 1 + levels)

    for j in range(nodes):
        turned[j] = bases_ref[j].T

    def project(j, step, carry):
        k = groups - 1 - step
        first = pl.multiple_of(flip(me, k) * share, share)
        piece = obs_ref[j * leaf : (j + 1) * leaf, pl.ds(first, share)]
        value = mm(turned[j], piece)

        @pl.when(k > 0)
        def _():
            send_a[j, k] = value
            copy_a(j, k).start()

        @pl.when(k == 0)
        def _():
            arrived[j][me] = value

        return carry

    for j in range(nodes):
        lax.fori_loop(0, groups, functools.partial(project, j), 0)

    def fold(step, carry):
        level = last - step // nodes
        j = step % nodes
        hot = lax.broadcasted_iota(jnp.int32, (rank, rank), 0) == perm_ref[level]
        far[level, j] = mm(transfer_ref[level, j, :, rank:], hot.astype(jnp.float32), 1)

        @pl.when(step == nodes - 1)
        def _():
            copy_w.start()

        return carry

    lax.fori_loop(0, levels * nodes, fold, 0)

    for j in range(nodes):
        for k in range(1, groups):
            copy_a(j, k).wait_recv()
        for k in list(range(1, groups)) + [0]:
            value = arrived[j][map_ref[flip(me, k), col]]
            if k:
                send_b[j, k] = value
                copy_b(j, k).start()
            else:
                cur[0, j, 0] = value

    pieces = nodes * groups

    def place(t):
        late = t - nodes
        own = (t < nodes).astype(jnp.int32)
        rest = 1 - own
        return own * t + rest * (late // (groups - 1)), rest * (1 + late % (groups - 1))

    delays = [0] + [1 + 2 * level for level in range(last)]

    def sweep(t, carry):
        @pl.when(t < pieces)
        def _():
            j, k = place(t)

            @pl.when(t >= nodes)
            def _():
                copy_b(j, k).wait_recv()

            copy_x(0, j, k).start()

        for level in range(last):
            back = delays[level + 1]

            @pl.when(jnp.logical_and(t >= back, t < pieces + back))
            def _():
                j, k = place(t - back)
                copy_x(level, j, k).wait_recv()
                value = mm(transfer_ref[level, j, :, :rank], cur[level, j, k]) + mm(
                    far[level, j], got[level, j, k]
                )
                if level < last - 1:
                    cur[level + 1, j, k] = value
                    copy_x(level + 1, j, k).start()
                else:

                    @pl.when(t == back)
                    def _():
                        copy_w.wait_recv()

                    send_r[0, j, k] = mm(far_away[j], value)

                    @pl.when(k > 0)
                    def _():
                        copy_r(0, j, k).start()

                    send_r[1, j, k] = mm(transfer_ref[last, j, :, :rank], value)

                    @pl.when(k > 0)
                    def _():
                        copy_r(1, j, k).start()

        return carry

    lax.fori_loop(0, pieces + delays[-1], sweep, 0)

    for j in range(nodes):
        value = send_r[0, j, 0]
        for k in range(1, groups):
            copy_r(0, j, k).wait_recv()
            value = value + got_r[0, j, k]
        send_f[j] = value
        copy_f(j).start()
    for j in range(nodes):
        value = send_r[1, j, 0]
        for k in range(1, groups):
            copy_r(1, j, k).wait_recv()
            value = value + got_r[1, j, k]
        copy_f(j).wait_recv()
        value = value + got_f[j]
        out_ref[:, j * leaf : (j + 1) * leaf] = mm(value.T, src_ref[j], 1)

    copy_w.wait_send()

    def drain(step, carry):
        j = step // groups
        k = step % groups
        for level in range(last):
            copy_x(level, j, k).wait_send()

        @pl.when(k > 0)
        def _():
            remote(
                send_a.at[j, k], send_b.at[j, k], sem_a, (j, k), over_obs(k)
            ).wait_send()
            copy_b(j, k).wait_send()
            copy_r(0, j, k).wait_send()
            copy_r(1, j, k).wait_send()

        @pl.when(k == 0)
        def _():
            copy_f(j).wait_send()

        return carry

    lax.fori_loop(0, nodes * groups, drain, 0)


def body(obs_field, observer_leaf_bases, transfer, src_basis, leaf_map, partner_perm):
    nodes, leaf, rank = observer_leaf_bases.shape
    levels = transfer.shape[0]
    last = levels - 1
    groups = lax.axis_size("obs")
    share = obs_field.shape[1] // groups
    block = (nodes, groups, rank, share)

    def buffer(*shape):
        return pltpu.VMEM(shape, jnp.float32)

    vmem = pl.BlockSpec(memory_space=pltpu.VMEM)
    dma = pltpu.SemaphoreType.DMA
    return pl.pallas_call(
        functools.partial(kernel, groups),
        out_shape=jax.ShapeDtypeStruct((share, nodes * leaf), jnp.float32),
        in_specs=[vmem] * 5 + [pl.BlockSpec(memory_space=pltpu.SMEM)],
        out_specs=vmem,
        scratch_shapes=[
            buffer(nodes, rank, leaf),
            buffer(levels, nodes, rank, rank),
            buffer(nodes, rank, rank),
            buffer(*block),
            buffer(*block),
            buffer(last, *block),
            buffer(last, *block),
            buffer(2, *block),
            buffer(2, *block),
            buffer(nodes, rank, share),
            buffer(nodes, rank, share),
            dma((2, 1)),
            dma((2, nodes, groups)),
            dma((2, nodes, groups)),
            dma((2, last, nodes, groups)),
            dma((2, 2, nodes, groups)),
            dma((2, nodes)),
        ]
        + [buffer(groups, rank, share)] * nodes,
        compiler_params=pltpu.CompilerParams(collective_id=0, has_side_effects=True),
    )(
        obs_field,
        observer_leaf_bases,
        transfer,
        src_basis,
        partner_perm.reshape(levels, 1, rank),
        leaf_map,
    )


def solution(mesh):
    placed = (
        P(("obs", "bfly"), None),
        P(("obs", "bfly"), None, None),
        P(None, ("obs", "bfly"), None, None),
        P("bfly", None, None),
        P(),
        P(),
    )
    return jax.shard_map(
        body, mesh=mesh, in_specs=placed, out_specs=P("obs", "bfly"), check_vma=False
    )
```

```python
import functools

import jax
import jax.numpy as jnp
from jax import lax
from jax.experimental import pallas as pl
from jax.experimental.pallas import tpu as pltpu
from jax.sharding import PartitionSpec as P

MESH = pl.DeviceIdType.MESH
EXACT = lax.Precision.HIGHEST


def mm(a, b, rhs_dim=0):
    return lax.dot_general(
        a,
        b,
        (((1,), (rhs_dim,)), ((), ())),
        precision=EXACT,
        preferred_element_type=jnp.float32,
    )


def flip(index, bits):
    out = index
    for shift in range(3):
        unit = 1 << shift
        out = out + unit * ((bits // unit) % 2) * (1 - 2 * ((index // unit) % 2))
    return out


def kernel(
    groups,
    obs_ref,
    bases_ref,
    transfer_ref,
    src_ref,
    perm_ref,
    map_ref,
    out_ref,
    turned,
    far,
    far_away,
    send_a,
    send_b,
    cur,
    got,
    send_r,
    got_r,
    send_f,
    got_f,
    sem_w,
    sem_a,
    sem_b,
    sem_x,
    sem_r,
    sem_f,
    *arrived,
):
    nodes, leaf, rank = bases_ref.shape
    levels = transfer_ref.shape[0]
    last = levels - 1
    share = obs_ref.shape[1] // groups
    me = lax.axis_index("obs")
    col = lax.axis_index("bfly")

    def over_obs(k):
        return (flip(me, k), col)

    def over_bfly(level):
        unit = 1 << level
        return (me, col + unit * (1 - 2 * ((col // unit) % 2)))

    def remote(src, dst, sems, index, device):
        return pltpu.make_async_remote_copy(
            src_ref=src,
            dst_ref=dst,
            send_sem=sems.at[(0, *index)],
            recv_sem=sems.at[(1, *index)],
            device_id=device,
            device_id_type=MESH,
        )

    def copy_a(j, k):
        return remote(send_a.at[j, k], arrived[j].at[me], sem_a, (j, k), over_obs(k))

    def copy_b(j, k):
        return remote(send_b.at[j, k], cur.at[0, j, k], sem_b, (j, k), over_obs(k))

    def copy_x(level, j, k):
        return remote(
            cur.at[level, j, k], got.at[level, j, k], sem_x, (level, j, k), over_bfly(level)
        )

    bits = [1 << i for i in range((groups - 1).bit_length())]
    hops, donors = [], []
    for ladder in (bits, bits[::-1]):
        hop = {k: next(bit for bit in ladder if k & bit) for k in range(1, groups)}
        hops.append(hop)
        donors.append(
            [[k for k in hop if k ^ hop[k] == chunk] for chunk in range(groups)]
        )

    def copy_r(which, j, k):
        return remote(
            send_r.at[which, j, k],
            got_r.at[which, j, k],
            sem_r,
            (which, j, k),
            over_obs(hops[which][k]),
        )

    def copy_f(j):
        return remote(send_f.at[j], got_f.at[j], sem_f, (j,), over_bfly(last))

    copy_w = remote(far.at[last], far_away, sem_w, (0,), over_bfly(last))

    barrier = pltpu.get_barrier_semaphore()
    for k in range(1, groups):
        pl.semaphore_signal(barrier, inc=1, device_id=over_obs(k), device_id_type=MESH)
    for level in range(levels):
        pl.semaphore_signal(barrier, inc=1, device_id=over_bfly(level), device_id_type=MESH)
    pl.semaphore_wait(barrier, groups - 1 + levels)

    for j in range(nodes):
        turned[j] = bases_ref[j].T

    def project(j, step, carry):
        k = groups - 1 - step
        first = pl.multiple_of(flip(me, k) * share, share)
        piece = obs_ref[j * leaf : (j + 1) * leaf, pl.ds(first, share)]
        value = mm(turned[j], piece)

        @pl.when(k > 0)
        def _():
            send_a[j, k] = value
            copy_a(j, k).start()

        @pl.when(k == 0)
        def _():
            arrived[j][me] = value

        return carry

    for j in range(nodes):
        lax.fori_loop(0, groups, functools.partial(project, j), 0)

    def fold(level, hot, j, carry):
        far[level, j] = mm(transfer_ref[level, j, :, rank:], hot, 1)
        return carry

    for level in range(last, -1, -1):
        rows = lax.broadcasted_iota(jnp.int32, (rank, rank), 0)
        hot = (rows == perm_ref[level : level + 1, :]).astype(jnp.float32)
        lax.fori_loop(0, nodes, functools.partial(fold, level, hot), 0)
        if level == last:
            copy_w.start()

    order = list(range(groups - 1, groups - 2, -1)) + list(range(1, groups - 1))

    def pick(j):
        for k in order:
            copy_a(j, k).wait_recv()
        for k in order + [0]:
            value = arrived[j][map_ref[flip(me, k), col]]
            if k:
                send_b[j, k] = value
                copy_b(j, k).start()
            else:
                cur[0, j, 0] = value

    pieces = nodes * groups

    def place(t):
        late = t - nodes
        own = (t < nodes).astype(jnp.int32)
        rest = 1 - own
        turn = late % (groups - 1)
        return (
            own * t + rest * (late // (groups - 1)),
            rest * (turn + (groups - 1) * (turn == 0).astype(jnp.int32)),
        )

    level_back = [1 + 2 * level for level in range(last)]
    far_back = level_back[-1]
    backs = (far_back, far_back + 3)

    def active(t, back):
        return jnp.logical_and(t >= back, t < pieces + back)

    def send_part(which, t):
        j, k = place(t)
        weights = far_away[j] if which == 0 else transfer_ref[last, j, :, :rank]
        send_r[which, j, k] = mm(weights, cur[last, j, k])

    def sweep(t, carry):
        for level in range(last):

            @pl.when(active(t, level_back[level]))
            def _():
                j, k = place(t - level_back[level])
                copy_x(level, j, k).wait_recv()
                value = mm(transfer_ref[level, j, :, :rank], cur[level, j, k]) + mm(
                    far[level, j], got[level, j, k]
                )
                cur[level + 1, j, k] = value
                if level < last - 1:
                    copy_x(level + 1, j, k).start()
                else:

                    @pl.when(t == far_back)
                    def _():
                        copy_w.wait_recv()

            if level == 0:
                for j in range(nodes):

                    @pl.when(t == j)
                    def _():
                        pick(j)

                @pl.when(t < pieces)
                def _():
                    j, k = place(t)

                    @pl.when(t >= nodes)
                    def _():
                        copy_b(j, k).wait_recv()

                    copy_x(0, j, k).start()

        for which in range(2):
            back = backs[which]

            @pl.when(active(t, back))
            def _():
                send_part(which, t - back)

            @pl.when(active(t, back))
            def _():
                j, k = place(t - back)

                @pl.when(k > 0)
                def _():
                    for chunk in range(1, groups):
                        if not donors[which][chunk]:

                            @pl.when(k == chunk)
                            def _():
                                copy_r(which, j, chunk).start()

            @pl.when(active(t, back + 1))
            def _():
                j, k = place(t - back - 1)
                for chunk in range(1, groups):
                    if donors[which][chunk]:

                        @pl.when(k == chunk)
                        def _():
                            for donor in donors[which][chunk]:
                                copy_r(which, j, donor).wait_recv()
                                send_r[which, j, chunk] += got_r[which, j, donor]
                            copy_r(which, j, chunk).start()

        return carry

    lax.fori_loop(0, pieces + backs[1] + 1, sweep, 0)

    for j in range(nodes):
        value = send_r[0, j, 0]
        for donor in donors[0][0]:
            copy_r(0, j, donor).wait_recv()
            value = value + got_r[0, j, donor]
        send_f[j] = value
        copy_f(j).start()
    for j in range(nodes):
        value = send_r[1, j, 0]
        for donor in donors[1][0]:
            copy_r(1, j, donor).wait_recv()
            value = value + got_r[1, j, donor]
        copy_f(j).wait_recv()
        value = value + got_f[j]
        out_ref[:, j * leaf : (j + 1) * leaf] = mm(value.T, src_ref[j], 1)

    copy_w.wait_send()

    def drain(step, carry):
        j = step // groups
        k = step % groups
        for level in range(last):
            copy_x(level, j, k).wait_send()

        @pl.when(k > 0)
        def _():
            remote(
                send_a.at[j, k], send_b.at[j, k], sem_a, (j, k), over_obs(k)
            ).wait_send()
            copy_b(j, k).wait_send()

        for chunk in range(1, groups):

            @pl.when(k == chunk)
            def _():
                for which in range(2):
                    copy_r(which, j, chunk).wait_send()

        @pl.when(k == 0)
        def _():
            copy_f(j).wait_send()

        return carry

    lax.fori_loop(0, nodes * groups, drain, 0)


def body(obs_field, observer_leaf_bases, transfer, src_basis, leaf_map, partner_perm):
    nodes, leaf, rank = observer_leaf_bases.shape
    levels = transfer.shape[0]
    last = levels - 1
    groups = lax.axis_size("obs")
    share = obs_field.shape[1] // groups
    block = (nodes, groups, rank, share)

    def buffer(*shape):
        return pltpu.VMEM(shape, jnp.float32)

    vmem = pl.BlockSpec(memory_space=pltpu.VMEM)
    dma = pltpu.SemaphoreType.DMA
    return pl.pallas_call(
        functools.partial(kernel, groups),
        out_shape=jax.ShapeDtypeStruct((share, nodes * leaf), jnp.float32),
        in_specs=[vmem] * 5 + [pl.BlockSpec(memory_space=pltpu.SMEM)],
        out_specs=vmem,
        scratch_shapes=[
            buffer(nodes, rank, leaf),
            buffer(levels, nodes, rank, rank),
            buffer(nodes, rank, rank),
            buffer(*block),
            buffer(*block),
            buffer(last + 1, *block),
            buffer(last, *block),
            buffer(2, *block),
            buffer(2, *block),
            buffer(nodes, rank, share),
            buffer(nodes, rank, share),
            dma((2, 1)),
            dma((2, nodes, groups)),
            dma((2, nodes, groups)),
            dma((2, last, nodes, groups)),
            dma((2, 2, nodes, groups)),
            dma((2, nodes)),
        ]
        + [buffer(groups, rank, share)] * nodes,
        compiler_params=pltpu.CompilerParams(collective_id=0, has_side_effects=True),
    )(
        obs_field,
        observer_leaf_bases,
        transfer,
        src_basis,
        partner_perm,
        leaf_map,
    )


def solution(mesh):
    placed = (
        P(("obs", "bfly"), None),
        P(("obs", "bfly"), None, None),
        P(None, ("obs", "bfly"), None, None),
        P("bfly", None, None),
        P(),
        P(),
    )
    return jax.shard_map(
        body, mesh=mesh, in_specs=placed, out_specs=P("obs", "bfly"), check_vma=False
    )
```

```python
import functools

import jax
import jax.numpy as jnp
from jax import lax
from jax.experimental import pallas as pl
from jax.experimental.pallas import tpu as pltpu
from jax.sharding import PartitionSpec as P

MESH = pl.DeviceIdType.MESH
EXACT = lax.Precision.HIGHEST


def mm(a, b, rhs_dim=0):
    return lax.dot_general(
        a,
        b,
        (((1,), (rhs_dim,)), ((), ())),
        precision=EXACT,
        preferred_element_type=jnp.float32,
    )


def flip(index, bits):
    out = index
    for shift in range(3):
        unit = 1 << shift
        out = out + unit * ((bits // unit) % 2) * (1 - 2 * ((index // unit) % 2))
    return out


def kernel(
    groups,
    obs_ref,
    bases_ref,
    transfer_ref,
    src_ref,
    perm_ref,
    map_ref,
    out_ref,
    turned,
    far,
    far_away,
    send_a,
    send_b,
    cur,
    got,
    send_r,
    got_r,
    send_f,
    got_f,
    sem_w,
    sem_a,
    sem_b,
    sem_x,
    sem_r,
    sem_f,
    *arrived,
):
    nodes, leaf, rank = bases_ref.shape
    levels = transfer_ref.shape[0]
    last = levels - 1
    share = obs_ref.shape[1] // groups
    me = lax.axis_index("obs")
    col = lax.axis_index("bfly")

    def over_obs(k):
        return (flip(me, k), col)

    def over_bfly(level):
        unit = 1 << level
        return (me, col + unit * (1 - 2 * ((col // unit) % 2)))

    def remote(src, dst, sems, index, device):
        return pltpu.make_async_remote_copy(
            src_ref=src,
            dst_ref=dst,
            send_sem=sems.at[(0, *index)],
            recv_sem=sems.at[(1, *index)],
            device_id=device,
            device_id_type=MESH,
        )

    def copy_a(j, k):
        return remote(send_a.at[j, k], arrived[j].at[me], sem_a, (j, k), over_obs(k))

    def copy_b(j, k):
        return remote(send_b.at[j, k], cur.at[0, j, k], sem_b, (j, k), over_obs(k))

    def copy_x(level, j, k):
        return remote(
            cur.at[level, j, k], got.at[level, j, k], sem_x, (level, j, k), over_bfly(level)
        )

    bits = [1 << i for i in range((groups - 1).bit_length())]
    hops, donors = [], []
    for ladder in (bits, bits[::-1]):
        hop = {k: next(bit for bit in ladder if k & bit) for k in range(1, groups)}
        hops.append(hop)
        donors.append(
            [[k for k in hop if k ^ hop[k] == chunk] for chunk in range(groups)]
        )

    def copy_r(which, j, k):
        return remote(
            send_r.at[which, j, k],
            got_r.at[which, j, k],
            sem_r,
            (which, j, k),
            over_obs(hops[which][k]),
        )

    def copy_f(j):
        return remote(send_f.at[j], got_f.at[j], sem_f, (j,), over_bfly(last))

    copy_w = remote(far.at[last], far_away, sem_w, (0,), over_bfly(last))

    barrier = pltpu.get_barrier_semaphore()
    for k in range(1, groups):
        pl.semaphore_signal(barrier, inc=1, device_id=over_obs(k), device_id_type=MESH)
    for level in range(levels):
        pl.semaphore_signal(barrier, inc=1, device_id=over_bfly(level), device_id_type=MESH)
    pl.semaphore_wait(barrier, groups - 1 + levels)

    for j in range(nodes):
        turned[j] = bases_ref[j].T

    def project(j, step, carry):
        k = groups - 1 - step
        first = pl.multiple_of(flip(me, k) * share, share)
        piece = obs_ref[j * leaf : (j + 1) * leaf, pl.ds(first, share)]
        value = mm(turned[j], piece)

        @pl.when(k > 0)
        def _():
            send_a[j, k] = value
            copy_a(j, k).start()

        @pl.when(k == 0)
        def _():
            arrived[j][me] = value

        return carry

    for j in range(nodes):
        lax.fori_loop(0, groups, functools.partial(project, j), 0)

    def fold(level, hot, j, carry):
        far[level, j] = mm(transfer_ref[level, j, :, rank:], hot, 1)
        return carry

    for level in range(last, -1, -1):
        rows = lax.broadcasted_iota(jnp.int32, (rank, rank), 0)
        hot = (rows == perm_ref[level : level + 1, :]).astype(jnp.float32)
        lax.fori_loop(0, nodes, functools.partial(fold, level, hot), 0)
        if level == last:
            copy_w.start()

    order = list(range(groups - 1, groups - 2, -1)) + list(range(1, groups - 1))

    def pick(j):
        for k in order:
            copy_a(j, k).wait_recv()
        for k in order + [0]:
            value = arrived[j][map_ref[flip(me, k), col]]
            if k:
                send_b[j, k] = value
                copy_b(j, k).start()
            else:
                cur[0, j, 0] = value

    pieces = nodes * groups

    def place(t):
        late = t - nodes
        own = (t < nodes).astype(jnp.int32)
        rest = 1 - own
        turn = late % (groups - 1)
        return (
            own * t + rest * (late // (groups - 1)),
            rest * (turn + (groups - 1) * (turn == 0).astype(jnp.int32)),
        )

    level_back = [1 + 3 * level for level in range(last)]
    far_back = level_back[-1]
    backs = (far_back, far_back)

    def active(t, back):
        return jnp.logical_and(t >= back, t < pieces + back)

    def send_part(which, t):
        j, k = place(t)
        weights = far_away[j] if which == 0 else transfer_ref[last, j, :, :rank]
        send_r[which, j, k] = mm(weights, cur[last, j, k])

    def sweep(t, carry):
        for level in range(last):

            @pl.when(active(t, level_back[level]))
            def _():
                j, k = place(t - level_back[level])
                copy_x(level, j, k).wait_recv()
                value = mm(transfer_ref[level, j, :, :rank], cur[level, j, k]) + mm(
                    far[level, j], got[level, j, k]
                )
                cur[level + 1, j, k] = value
                if level < last - 1:
                    copy_x(level + 1, j, k).start()
                else:

                    @pl.when(t == far_back)
                    def _():
                        copy_w.wait_recv()

            if level == 0:
                for j in range(nodes):

                    @pl.when(t == j)
                    def _():
                        pick(j)

                @pl.when(t < pieces)
                def _():
                    j, k = place(t)

                    @pl.when(t >= nodes)
                    def _():
                        copy_b(j, k).wait_recv()

                    copy_x(0, j, k).start()

        for which in range(2):
            back = backs[which]

            @pl.when(active(t, back))
            def _():
                send_part(which, t - back)

            @pl.when(active(t, back))
            def _():
                j, k = place(t - back)

                @pl.when(k > 0)
                def _():
                    for chunk in range(1, groups):
                        if not donors[which][chunk]:

                            @pl.when(k == chunk)
                            def _():
                                copy_r(which, j, chunk).start()

            @pl.when(active(t, back + 1))
            def _():
                j, k = place(t - back - 1)
                for chunk in range(1, groups):
                    if donors[which][chunk]:

                        @pl.when(k == chunk)
                        def _():
                            for donor in donors[which][chunk]:
                                copy_r(which, j, donor).wait_recv()
                                send_r[which, j, chunk] += got_r[which, j, donor]
                            copy_r(which, j, chunk).start()

        return carry

    lax.fori_loop(0, pieces + backs[1] + 1, sweep, 0)

    for j in range(nodes):
        value = send_r[0, j, 0]
        for donor in donors[0][0]:
            copy_r(0, j, donor).wait_recv()
            value = value + got_r[0, j, donor]
        send_f[j] = value
        copy_f(j).start()
    for j in range(nodes):
        value = send_r[1, j, 0]
        for donor in donors[1][0]:
            copy_r(1, j, donor).wait_recv()
            value = value + got_r[1, j, donor]
        copy_f(j).wait_recv()
        value = value + got_f[j]
        out_ref[:, j * leaf : (j + 1) * leaf] = mm(value.T, src_ref[j], 1)

    copy_w.wait_send()

    def drain(step, carry):
        j = step // groups
        k = step % groups
        for level in range(last):
            copy_x(level, j, k).wait_send()

        @pl.when(k > 0)
        def _():
            remote(
                send_a.at[j, k], send_b.at[j, k], sem_a, (j, k), over_obs(k)
            ).wait_send()
            copy_b(j, k).wait_send()

        for chunk in range(1, groups):

            @pl.when(k == chunk)
            def _():
                for which in range(2):
                    copy_r(which, j, chunk).wait_send()

        @pl.when(k == 0)
        def _():
            copy_f(j).wait_send()

        return carry

    lax.fori_loop(0, nodes * groups, drain, 0)


def body(obs_field, observer_leaf_bases, transfer, src_basis, leaf_map, partner_perm):
    nodes, leaf, rank = observer_leaf_bases.shape
    levels = transfer.shape[0]
    last = levels - 1
    groups = lax.axis_size("obs")
    share = obs_field.shape[1] // groups
    block = (nodes, groups, rank, share)

    def buffer(*shape):
        return pltpu.VMEM(shape, jnp.float32)

    vmem = pl.BlockSpec(memory_space=pltpu.VMEM)
    dma = pltpu.SemaphoreType.DMA
    return pl.pallas_call(
        functools.partial(kernel, groups),
        out_shape=jax.ShapeDtypeStruct((share, nodes * leaf), jnp.float32),
        in_specs=[vmem] * 5 + [pl.BlockSpec(memory_space=pltpu.SMEM)],
        out_specs=vmem,
        scratch_shapes=[
            buffer(nodes, rank, leaf),
            buffer(levels, nodes, rank, rank),
            buffer(nodes, rank, rank),
            buffer(*block),
            buffer(*block),
            buffer(last + 1, *block),
            buffer(last, *block),
            buffer(2, *block),
            buffer(2, *block),
            buffer(nodes, rank, share),
            buffer(nodes, rank, share),
            dma((2, 1)),
            dma((2, nodes, groups)),
            dma((2, nodes, groups)),
            dma((2, last, nodes, groups)),
            dma((2, 2, nodes, groups)),
            dma((2, nodes)),
        ]
        + [buffer(groups, rank, share)] * nodes,
        compiler_params=pltpu.CompilerParams(collective_id=0, has_side_effects=True),
    )(
        obs_field,
        observer_leaf_bases,
        transfer,
        src_basis,
        partner_perm,
        leaf_map,
    )


def solution(mesh):
    placed = (
        P(("obs", "bfly"), None),
        P(("obs", "bfly"), None, None),
        P(None, ("obs", "bfly"), None, None),
        P("bfly", None, None),
        P(),
        P(),
    )
    return jax.shard_map(
        body, mesh=mesh, in_specs=placed, out_specs=P("obs", "bfly"), check_vma=False
    )
```
